256 devices in a mesh: sub: 64 (over x, z, core), grp: 4 (over y).
Axes of the slice: x: 4, y: 4, z: 8, core: 2. Of those that a mesh axis runs over, the one named last changes fastest.
Arguments:
- right_side: float32 [524288, 128], P(('sub', 'grp')), may hold values from -6 to 6
- noise_var: float32 [524288], P(('sub', 'grp')), may hold values from 0.5 to 2
- near_tiles: bfloat16 [2048, 6, 256, 256], P(('sub', 'grp')), may hold values from -0.15625 to 0.15625
- near_index: int32 [2048, 6], P(('sub', 'grp')), may hold values from 0 to 2047, as said below
- leaf_basis: bfloat16 [2048, 64, 256], P(('sub', 'grp')), may hold values from -0.375 to 0.375
- leaf_transfer: bfloat16 [2048, 64, 64], P(('sub', 'grp')), may hold values from -0.4375 to 0.4375
- leaf_coupling: bfloat16 [2048, 4, 64, 64], P(('sub', 'grp')), may hold values from -0.375 to 0.375
- far_leaf: int32 [2048, 4], P(('sub', 'grp')), may hold values from 0 to 2047, as said below
- dev_transfer: bfloat16 [256, 64, 64], P(('sub', 'grp')), may hold values from -0.4375 to 0.4375
- dev_coupling: bfloat16 [256, 4, 64, 64], P(('sub', 'grp')), may hold values from -0.375 to 0.375
- far_dev: int32 [256, 4], P(('sub', 'grp')), may hold values from 0 to 255, as said below
- mid_coupling: bfloat16 [32, 3, 64, 64], P('grp'), may hold values from -0.4375 to 0.4375
- far_mid: int32 [32, 3], P('grp'), may hold values from 0 to 31, as said below
Outputs:
- solution: float32 [524288, 128], P(('sub', 'grp'))
The draws below stay inside these ranges and needn't reach their ends.
Inputs may be any that keep to these rules, and one draw needn't show every extreme that they name: `near_index`: row l lists 6 different leaves, l itself among them, each within 6 leaves of l in the periodic leaf order (leaf indices taken modulo 2048). `far_leaf`: row l lists 4 different leaves within 6 leaves of l in the periodic leaf order, none of them in row l of near_index. `far_dev`: row d lists 4 different subtrees other than d, each of the same group as d. `far_mid`: row m lists 3 different mid nodes other than m.
All inputs are finite; a program needn't handle non-finite values.
Results may differ from the reference program's by a relative error of at most 0.025.
Values may be sent and summed in bfloat16 or wider, within the bound.
No kernel may reach another device: no remote copies, remote signals or barrier semaphores. Data moves between devices by JAX's collectives and lax.ppermute only.
A program may use at most 64 MiB of HBM per device.

```python
import math
import jax
import jax.numpy as jnp
from jax import lax

LEAF = 256
RANK = 64
PROBES = 128
LEAVES_DEV = 8
NEAR = 6
FAR_LEAF = 4
SPAN = 6
FAR_DEV = 4
FAR_MID = 3
ITERS = 4
GROUPS = 4
GROUP_DEVS = 64
MID_GRP = 8
MIDS = 32
SUBTREES = 256
LEAVES = 2048
ROWS = 524288


def leaf_lists(key):
    inner = jax.random.fold_in(key, 11)
    width = 2 * SPAN + 1
    scores = jax.random.randint(inner, (LEAVES, width), 0, 1 << 20) * 64 + jnp.arange(width, dtype=jnp.int32)[None, :]
    scores = scores.at[:, SPAN].set(-1)
    order = jnp.argsort(scores, axis=1, stable=True)[:, :NEAR + FAR_LEAF].astype(jnp.int32)
    offsets = order - SPAN
    leaf_ids = jnp.arange(LEAVES, dtype=jnp.int32)[:, None]
    return jnp.mod(leaf_ids + offsets, LEAVES).astype(jnp.int32)


def draw_near_index(key, part):
    return leaf_lists(key)[:, :NEAR]


def draw_far_leaf(key, part):
    return leaf_lists(key)[:, NEAR:]


def draw_far_dev(key, part):
    inner = jax.random.fold_in(key, 23)
    scores = jax.random.randint(inner, (SUBTREES, GROUP_DEVS), 0, 1 << 20) * 128 + jnp.arange(GROUP_DEVS, dtype=jnp.int32)[None, :]
    dev_ids = jnp.arange(SUBTREES, dtype=jnp.int32)
    within = dev_ids // GROUPS
    group_of = dev_ids % GROUPS
    columns = jnp.arange(GROUP_DEVS, dtype=jnp.int32)[None, :]
    scores = jnp.where(columns == within[:, None], 1 << 30, scores)
    forced = (within[:, None] == 0) & (columns == GROUP_DEVS - 1) | (within[:, None] == GROUP_DEVS - 1) & (columns == 0)
    scores = jnp.where(forced, -1, scores)
    order = jnp.argsort(scores, axis=1, stable=True)[:, :FAR_DEV].astype(jnp.int32)
    return (order * GROUPS + group_of[:, None]).astype(jnp.int32)


def draw_far_mid(key, part):
    inner = jax.random.fold_in(key, 37)
    scores = jax.random.randint(inner, (MIDS, MIDS), 0, 1 << 20) * 128 + jnp.arange(MIDS, dtype=jnp.int32)[None, :]
    mid_ids = jnp.arange(MIDS, dtype=jnp.int32)[:, None]
    columns = jnp.arange(MIDS, dtype=jnp.int32)[None, :]
    scores = jnp.where(columns == mid_ids, 1 << 30, scores)
    forced = (mid_ids == 0) & (columns == MIDS - 1) | (mid_ids == MIDS - 1) & (columns == 0)
    scores = jnp.where(forced, -1, scores)
    return jnp.argsort(scores, axis=1, stable=True)[:, :FAR_MID].astype(jnp.int32)


def shard_levels(key, extent, cuts, smallest, largest):
    level, own = 1.0, jax.random.fold_in(key, 6)
    for dim, blocks in cuts:
        heights = jnp.exp(jax.random.uniform(jax.random.fold_in(own, dim), (blocks,), jnp.float32, smallest / len(cuts), largest / len(cuts)))
        level = level * jnp.repeat(heights, extent[dim] // blocks).reshape([-1 if axis == dim else 1 for axis in range(len(extent))])
    return level


def noise(stream_key, dims, deviation, most, shards=(), kind=jnp.bfloat16):
    factor_of = shard_levels(stream_key, dims, shards, -0.22, 0.18) if shards else 1.0
    result = jax.random.normal(stream_key, dims, jnp.float32) * deviation * factor_of
    return jnp.minimum(jnp.maximum(result, -most), most).astype(kind)


def setup_inputs(seed: int = 0) -> dict:
    key_list = jax.random.split(jax.random.key(seed), 14)
    return {
        "right_side": noise(key_list[0], (ROWS, PROBES), 1.0, 6.0, ((0, 256),), jnp.float32),
        "noise_var": jnp.clip(jnp.exp(math.log(2.0) - 1.3862944 * jax.random.uniform(key_list[1], (ROWS,), jnp.float32) ** shard_levels(key_list[1], (ROWS,), ((0, 256),), -0.2, 0.2)), 0.5, 2.0),
        "near_tiles": noise(key_list[2], (LEAVES, NEAR, LEAF, LEAF), (LEAF * NEAR) ** -0.5, 0.15625, ((0, 256),)),
        "near_index": draw_near_index(jax.random.fold_in(key_list[13], 71), 0),
        "leaf_basis": noise(key_list[4], (LEAVES, RANK, LEAF), LEAF ** -0.5, 0.375, ((0, 256),)),
        "leaf_transfer": noise(key_list[5], (LEAVES, RANK, RANK), (3 * RANK) ** -0.5, 0.4375, ((0, 256),)),
        "leaf_coupling": noise(key_list[6], (LEAVES, FAR_LEAF, RANK, RANK), (RANK * FAR_LEAF) ** -0.5, 0.375, ((0, 256),)),
        "far_leaf": draw_far_leaf(jax.random.fold_in(key_list[13], 71), 0),
        "dev_transfer": noise(key_list[8], (SUBTREES, RANK, RANK), (3 * RANK) ** -0.5, 0.4375, ((0, 256),)),
        "dev_coupling": noise(key_list[9], (SUBTREES, FAR_DEV, RANK, RANK), (RANK * FAR_DEV) ** -0.5, 0.375, ((0, 256),)),
        "far_dev": draw_far_dev(jax.random.fold_in(key_list[13], 71), 0),
        "mid_coupling": noise(key_list[11], (MIDS, FAR_MID, RANK, RANK), (RANK * FAR_MID) ** -0.5, 0.4375, ((0, 4),)),
        "far_mid": draw_far_mid(jax.random.fold_in(key_list[13], 71), 0),
    }


relax_step = 0.3


def operate(iterate, noise_var, near_tiles, near_index, leaf_basis, leaf_transfer, leaf_coupling, far_leaf, dev_transfer, dev_coupling, far_dev, mid_coupling, far_mid):
    rounded = iterate.astype(jnp.bfloat16).reshape(LEAVES, LEAF, PROBES)
    basis32 = leaf_basis.astype(jnp.float32)
    ltrans32 = leaf_transfer.astype(jnp.float32)
    dtrans32 = dev_transfer.astype(jnp.float32)
    leaf_coef = jnp.einsum("lrj,ljp->lrp", basis32, rounded.astype(jnp.float32)).astype(jnp.bfloat16)
    dev_terms = jnp.einsum("lrs,lsp->lrp", ltrans32, leaf_coef.astype(jnp.float32))
    dev_coef = dev_terms.reshape(SUBTREES, LEAVES_DEV, RANK, PROBES).sum(1).astype(jnp.bfloat16)
    lifted = jnp.einsum("drs,dsp->drp", dtrans32, dev_coef.astype(jnp.float32)).astype(jnp.bfloat16)
    grouped = lifted.astype(jnp.float32).reshape(MID_GRP, 8, GROUPS, RANK, PROBES).sum(1)
    mid_coef = jnp.transpose(grouped, (1, 0, 2, 3)).reshape(MIDS, RANK, PROBES).astype(jnp.bfloat16)
    mid_field = jnp.einsum("mkrs,mksp->mrp", mid_coupling.astype(jnp.float32), mid_coef[far_mid].astype(jnp.float32)).astype(jnp.bfloat16)
    dev_ids = jnp.arange(SUBTREES, dtype=jnp.int32)
    parent = (dev_ids % GROUPS) * MID_GRP + (dev_ids // GROUPS) // 8
    dev_field = jnp.einsum("dkrs,dksp->drp", dev_coupling.astype(jnp.float32), dev_coef[far_dev].astype(jnp.float32))
    dev_field = dev_field + jnp.einsum("drs,drp->dsp", dtrans32, mid_field[parent].astype(jnp.float32))
    dev_field = dev_field.astype(jnp.bfloat16)
    spread = jnp.repeat(dev_field, LEAVES_DEV, axis=0).astype(jnp.float32)
    leaf_field = jnp.einsum("lkrs,lksp->lrp", leaf_coupling.astype(jnp.float32), leaf_coef[far_leaf].astype(jnp.float32))
    leaf_field = (leaf_field + jnp.einsum("lrs,lrp->lsp", ltrans32, spread)).astype(jnp.bfloat16)
    far_part = jnp.einsum("lrj,lrp->ljp", basis32, leaf_field.astype(jnp.float32))

    def near_block(pieces):
        tiles, indices = pieces
        gathered = rounded[indices].astype(jnp.float32)
        return jnp.einsum("lkij,lkjp->lip", tiles.astype(jnp.float32), gathered)

    near_part = lax.map(near_block, (near_tiles.reshape(SUBTREES, LEAVES_DEV, NEAR, LEAF, LEAF), near_index.reshape(SUBTREES, LEAVES_DEV, NEAR)))
    total = near_part.reshape(LEAVES, LEAF, PROBES) + far_part
    return total.reshape(ROWS, PROBES) + noise_var[:, None] * iterate


def reference(right_side, noise_var, near_tiles, near_index, leaf_basis, leaf_transfer, leaf_coupling, far_leaf, dev_transfer, dev_coupling, far_dev, mid_coupling, far_mid):
    iterate = relax_step * right_side
    for sweep in range(ITERS):
        image = operate(iterate, noise_var, near_tiles, near_index, leaf_basis, leaf_transfer, leaf_coupling, far_leaf, dev_transfer, dev_coupling, far_dev, mid_coupling, far_mid)
        iterate = iterate + relax_step * (right_side - image)
    return iterate
```

```python
import functools

import jax
import jax.numpy as jnp
from jax import lax
from jax.experimental import pallas as pl
from jax.experimental.pallas import tpu as pltpu
from jax.sharding import Mesh
from jax.sharding import PartitionSpec as P

SPAN = 6
ITERS = 4
NX, NZ, NC, NY = 4, 8, 2, 4
ALL = ("x", "z", "c", "y")
relax_step = 0.3
bf16, f32, i32 = jnp.bfloat16, jnp.float32, jnp.int32


def from_behind(value, axis, steps):
    count = lax.axis_size(axis)
    pairs = [(source, (source + steps) % count) for source in range(count)]
    return lax.ppermute(value, axis, pairs)


def exchange(chunks, axes):
    return lax.all_to_all(chunks, axes, split_axis=0, concat_axis=0, tiled=True)


def dot(a, b):
    return jnp.dot(a, b, preferred_element_type=f32)


def dot_t(a, b):
    return lax.dot_general(a, b, (((0,), (0,)), ((), ())), preferred_element_type=f32)


def whole(*dims):
    return pl.BlockSpec(dims, lambda *_: (0,) * len(dims))


VMEM = pl.BlockSpec(memory_space=pltpu.VMEM)
HBM = pl.BlockSpec(memory_space=pltpu.HBM)


def in_hbm(*arrays):
    return [pltpu.with_memory_space_constraint(a, pltpu.HBM) for a in arrays]


def in_vmem(*arrays):
    return [pltpu.with_memory_space_constraint(a, pltpu.VMEM) for a in arrays]


def hbm_out(dims, kind=bf16):
    return pltpu.HBM(dims, kind)


def vmem_out(dims, kind=bf16):
    return pltpu.VMEM(dims, kind)


def setup_kernel(index_ref, transfer_ref, coupling_ref, mid_ref, out_ref):
    lane = lax.broadcasted_iota(i32, (64, 128), 1)
    t = transfer_ref[0]
    folded = [dot_t(t, mid_ref[0, k]) for k in range(3)]
    c = [coupling_ref[0, k].astype(f32) for k in range(4)]
    codes = jnp.zeros((64, 128), f32)
    for i in range(7):
        codes = jnp.where(lane == 64 + i, index_ref[1 + i].astype(f32), codes)
    slots = [
        jnp.concatenate([c[0], c[1]], 1),
        jnp.concatenate([c[2], c[3]], 1),
        jnp.concatenate([folded[0], folded[1]], 1),
        jnp.where(lane < 64, jnp.concatenate([folded[2], folded[2]], 1), codes),
    ]
    slots = [s.astype(bf16) for s in slots]
    for q in range(NX * NY):
        for i in range(4):
            out_ref[q, i] = slots[i]


def weights_kernel(place_ref, index_ref, got_ref, wd_ref, wm_ref):
    lane = lax.broadcasted_iota(i32, (64, 128), 1)
    x, y = place_ref[0], place_ref[1]
    wd_ref[...] = jnp.zeros_like(wd_ref)
    wm_ref[...] = jnp.zeros_like(wm_ref)

    def half(value, source, target):
        swapped = jnp.concatenate([value[:, 64:], value[:, :64]], 1)
        moved = jnp.where(target == source, value, swapped)
        return jnp.where(lane // 64 == target, moved, 0.0)

    for xd in range(NX):
        q = xd * NY + y
        for k in range(4):
            sub = index_ref[q * 8 + k]

            @pl.when(sub // (NZ * NC) == x)
            def _(sub=sub, q=q, k=k, xd=xd):
                zf = lax.rem(sub // NC, NZ)
                value = half(got_ref[q, k // 2].astype(f32), k % 2, lax.rem(sub, NC))
                rows = pl.ds(xd * 64, 64)
                wd_ref[zf, rows, :] = (wd_ref[zf, rows, :].astype(f32) + value).astype(bf16)

    def mids(q, carry):
        for k in range(3):
            m = index_ref[q * 8 + 4 + k]

            @pl.when(m // 2 == y * NX + x)
            def _(m=m, k=k):
                value = half(got_ref[q, 2 + k // 2].astype(f32), k % 2, lax.rem(m, 2))
                wm_ref[q] = (wm_ref[q].astype(f32) + value).astype(bf16)

        return carry

    lax.fori_loop(0, NX * NY, mids, 0)


def coefficients(rounded, l, basis_ref, ltrans_ref, coef_ref):
    coef = dot(basis_ref[l], rounded).astype(bf16)
    coef_ref[l] = coef
    return dot(ltrans_ref[l], coef)


def first_kernel(
    place_ref, rhs_ref, basis_ref, ltrans_ref, dtrans_ref,
    x_ref, right_ref, left_ref, coef_ref, stage_ref,
):
    total = jnp.zeros((64, 128), f32)
    for l in range(8):
        value = relax_step * rhs_ref[l]
        x_ref[l] = value
        rounded = value.astype(bf16)
        halves = (basis_ref[l, :, :128], basis_ref[l, :, 128:])
        for ref, at in ((right_ref, l - 2), (left_ref, l)):
            if 0 <= at < SPAN:
                ref[at, 0:256, :] = rounded
                ref[at, 256:320, :] = halves[0]
                ref[at, 320:384, :] = halves[1]
        total = total + coefficients(rounded, l, basis_ref, ltrans_ref, coef_ref)
    dev_coef = total.astype(bf16)
    lane = lax.broadcasted_iota(i32, (64, 128), 1)
    t = dtrans_ref[0].astype(f32)
    t = jnp.where(lane // 64 == place_ref[3], jnp.concatenate([t, t], 1), 0.0).astype(bf16)
    for j in range(NZ * NC):
        stage_ref[j, 0:64, :] = dev_coef
        stage_ref[j, 64:128, :] = t


def copies_of(pairs, sems):
    made = [pltpu.make_async_copy(a, b, sems.at[i]) for i, (a, b) in enumerate(pairs)]
    for c in made:
        c.start()
    return made


def spread_kernel(
    place_ref, got, tz_hbm, wd_hbm, wm_hbm, out_hbm, tz, wd, wm, total, out, sems
):
    copies = copies_of([(tz_hbm, tz), (wd_hbm, wd), (wm_hbm, wm)], sems)
    for c in copies[:2]:
        c.wait()
    halves, dev = [], None
    for zh in range(2):
        mid = None
        for z in range(4 * zh, 4 * zh + 4):
            g = jnp.concatenate([got[2 * z, 0:64, :], got[2 * z + 1, 0:64, :]], 0)
            part = dot(tz[z], g)
            mid = part if mid is None else mid + part
            part = dot(wd[z], g)
            dev = part if dev is None else dev + part
        halves.append(mid.astype(bf16))
    copies[2].wait()
    value = dot(wm[...].reshape(1024, 128), jnp.concatenate(halves, 0)).reshape(16, 64, 128)
    total[...] = value
    out[...] = value.astype(bf16)
    y = place_ref[1]
    for xd in range(NX):
        q = xd * NY + y
        out[q] = (total[q] + dev[xd * 64 : xd * 64 + 64, :]).astype(bf16)
    c = pltpu.make_async_copy(out, out_hbm, sems.at[3])
    c.start()
    c.wait()


def near_kernel(
    near_ref, far_ref, below_ref, above_ref, x_ref, tiles_hbm, rhs_hbm, noise_hbm, coupling_hbm,
    right_hbm, left_hbm, basis_b_hbm, basis_a_hbm, coef_hbm, base_ref, pre_ref,
    tiles, rhs, noise, coupling, window, basis, wcoef, sems, leaf_sems,
):
    vec = pl.ds(0, 256)
    copies = copies_of(
        [
            (below_ref.at[:, vec, :], window.at[0:SPAN]),
            (left_hbm.at[:, vec, :], window.at[SPAN : 2 * SPAN]),
            (right_hbm.at[SPAN - 2 : SPAN, vec, :], window.at[2 * SPAN : SPAN + 8]),
            (above_ref.at[:, vec, :], window.at[SPAN + 8 : 2 * SPAN + 8]),
            (basis_b_hbm, basis.at[0:SPAN]),
            (basis_a_hbm, basis.at[SPAN : 2 * SPAN]),
            (coef_hbm, wcoef.at[SPAN : SPAN + 8]),
            (noise_hbm, noise),
            (coupling_hbm, coupling),
        ],
        sems,
    )

    def leaf_copies(l):
        pairs = ((tiles_hbm, tiles), (rhs_hbm, rhs))
        return [pltpu.make_async_copy(a.at[l], b.at[l], leaf_sems.at[i, l]) for i, (a, b) in enumerate(pairs)]

    for l in range(2):
        for c in leaf_copies(l):
            c.start()
    for c in copies:
        c.wait()
    for i in range(2 * SPAN):
        at = i if i < SPAN else i + 8
        v, b = window[at], basis[i]
        wcoef[at] = (dot(b[0:64, :], v[:128]) + dot(b[64:128, :], v[128:])).astype(bf16)

    def leaf(l, carry):
        part = None
        for k in range(4):
            more = dot(coupling[l, k], wcoef[far_ref[l * 4 + k]])
            part = more if part is None else part + more
        pre_ref[l] = part
        @pl.when(l + 2 < 8)
        def _():
            for c in leaf_copies(l + 2):
                c.start()

        for c in leaf_copies(l):
            c.wait()
        near = dot(
            jnp.concatenate([tiles[l, k] for k in range(6)], 1),
            jnp.concatenate([window[near_ref[l * 6 + k]] for k in range(6)], 0),
        )
        scale = noise[l]
        for h in range(2):
            rows = pl.ds(h * 128, 128)
            column = jnp.broadcast_to(scale[h : h + 1, :], (128, 128)).T
            value = x_ref[l, rows, :]
            image = near[h * 128 : h * 128 + 128, :] + column * value
            base_ref[l, rows, :] = value + relax_step * (rhs[l, rows, :] - image)
        return carry

    lax.fori_loop(0, 8, leaf, 0)


def corrected(got, base, pre, basis_t_hbm, ltrans_t_hbm, basis_t, ltrans_t, sems, more):
    pairs = [(ltrans_t_hbm, ltrans_t), (basis_t_hbm, basis_t)] + more
    copies = copies_of(pairs, sems)
    total = got[0].astype(f32)
    for q in range(1, NX * NY):
        total = total + got[q].astype(f32)
    for c in copies:
        c.wait()
    leaf = (pre[...].reshape(512, 128) + dot(ltrans_t[...], total.astype(bf16))).astype(bf16)
    zero = jnp.zeros((64, 128), bf16)
    for l in range(8):
        own = leaf[64 * l : 64 * l + 64, :]
        pair = jnp.concatenate([own, zero] if l % 2 == 0 else [zero, own], 0)
        yield l, base[l] - relax_step * dot(basis_t[l // 2], pair)


def update_kernel(
    got, base, pre, basis_t_hbm, ltrans_t_hbm, basis_hbm, ltrans_hbm,
    x_ref, right_hbm, left_hbm, coef_hbm, stage_hbm,
    basis_t, ltrans_t, basis, ltrans, rounded, coef, dev, sems, out_sems,
):
    outs = []

    def send(a, b):
        c = pltpu.make_async_copy(a, b, out_sems.at[len(outs)])
        c.start()
        outs.append(c)

    values = corrected(
        got, base, pre, basis_t_hbm, ltrans_t_hbm, basis_t, ltrans_t, sems,
        [(basis_hbm, basis), (ltrans_hbm, ltrans)],
    )
    for l, value in values:
        x_ref[l] = value
        rounded[l] = value.astype(bf16)
        if l == 3:
            send(rounded.at[0:4], left_hbm.at[0:4])
            send(rounded.at[2:4], right_hbm.at[0:2])
    send(rounded.at[4:6], left_hbm.at[4:6])
    send(rounded.at[4:8], right_hbm.at[2:6])
    for l in range(8):
        coef[l] = dot(basis[l], rounded[l]).astype(bf16)
    dev[...] = dot(ltrans[...], coef[...].reshape(512, 128)).astype(bf16)
    for j in range(NZ * NC):
        send(dev, stage_hbm.at[j])
    send(coef, coef_hbm)
    for c in outs:
        c.wait()


def last_kernel(
    got, base, pre, basis_t_hbm, ltrans_t_hbm, x_hbm, x, basis_t, ltrans_t, sems, out_sems
):
    outs = []
    for l, value in corrected(got, base, pre, basis_t_hbm, ltrans_t_hbm, basis_t, ltrans_t, sems, []):
        x[l] = value
        if l % 2:
            pair = pl.ds(l - 1, 2)
            outs.append(pltpu.make_async_copy(x.at[pair], x_hbm.at[pair], out_sems.at[l // 2]))
            outs[-1].start()
    for c in outs:
        c.wait()


LOADED = [pltpu.VMEM((4, 256, 128), bf16), pltpu.VMEM((512, 64), bf16)]
DMAS = pltpu.SemaphoreType.DMA


def shape(dims, kind=bf16):
    return jax.ShapeDtypeStruct(dims, kind)


LIMIT = pltpu.CompilerParams(vmem_limit_bytes=24 << 20)
SMEM = pl.BlockSpec(memory_space=pltpu.SMEM)


def per_device(
    right_side, noise_var, near_tiles, near_index, leaf_basis, leaf_transfer, leaf_coupling,
    far_leaf, dev_transfer, dev_coupling, far_dev, mid_coupling, far_mid,
):
    xi, zi, ci, yi = (lax.axis_index(a) for a in ALL)
    sub = (xi * NZ + zi) * NC + ci
    device = sub * NY + yi
    total_leaves = 8 * NX * NZ * NC * NY
    first_leaf = device * 8
    near_local = jnp.mod(near_index - first_leaf + SPAN, total_leaves).reshape(-1)
    far_local = jnp.mod(far_leaf - first_leaf + SPAN, total_leaves).reshape(-1)
    place = jnp.stack([xi, yi, zi, ci]).astype(i32)
    mid_local = sub // 8
    own_far_mid = lax.dynamic_index_in_dim(far_mid, mid_local, 0, keepdims=False)
    codes = jnp.concatenate([mid_local[None].astype(i32), far_dev[0] // NY, own_far_mid])
    rhs = right_side.reshape(8, 256, 128)
    noise = noise_var.reshape(8, 2, 128)
    basis_t = leaf_basis.reshape(4, 128, 256).swapaxes(1, 2)
    ltrans_t = leaf_transfer.swapaxes(1, 2).reshape(512, 64)
    ltrans = leaf_transfer.swapaxes(0, 1).reshape(64, 512)

    setup = pl.pallas_call(
        setup_kernel,
        out_shape=shape((16, 4, 64, 128)),
        grid_spec=pltpu.PrefetchScalarGridSpec(
            num_scalar_prefetch=1,
            grid=(1,),
            in_specs=[
                pl.BlockSpec((1, 64, 64), lambda i, s: (0, 0, 0)),
                pl.BlockSpec((1, 4, 64, 64), lambda i, s: (0, 0, 0, 0)),
                pl.BlockSpec((1, 3, 64, 64), lambda i, s: (s[0], 0, 0, 0)),
            ],
            out_specs=pl.BlockSpec((16, 4, 64, 128), lambda i, s: (0, 0, 0, 0)),
        ),
        cost_estimate=pl.CostEstimate(flops=4_000_000, bytes_accessed=1_200_000, transcendentals=0),
    )(codes, dev_transfer, dev_coupling, mid_coupling)

    x, right, left, coef, stage = pl.pallas_call(
        first_kernel,
        out_shape=(
            shape((8, 256, 128), f32), shape((SPAN, 384, 128)),
            shape((SPAN, 384, 128)), shape((8, 64, 128)), shape((16, 128, 128)),
        ),
        grid=(1,),
        in_specs=[SMEM, whole(8, 256, 128), whole(8, 64, 256), whole(8, 64, 64), whole(1, 64, 64)],
        out_specs=[
            whole(8, 256, 128), whole(SPAN, 384, 128), whole(SPAN, 384, 128), whole(8, 64, 128),
            whole(16, 128, 128),
        ],
        cost_estimate=pl.CostEstimate(flops=42_000_000, bytes_accessed=4_500_000, transcendentals=0),
    )(place, rhs, leaf_basis, leaf_transfer, dev_transfer)

    got_setup = exchange(setup, ("x", "y"))
    weights_in = got_setup[:, 3, 0, 64:72].astype(f32).astype(i32).reshape(-1)
    wd, wm = pl.pallas_call(
        weights_kernel,
        out_shape=(shape((8, 256, 128)), shape((16, 64, 128))),
        grid=(1,),
        in_specs=[SMEM, SMEM, whole(16, 4, 64, 128)],
        out_specs=[whole(8, 256, 128), whole(16, 64, 128)],
        cost_estimate=pl.CostEstimate(flops=1_000_000, bytes_accessed=2_000_000, transcendentals=0),
    )(place, weights_in, got_setup)

    basis_b = basis_a = tz = None
    for sweep in range(ITERS):
        below = from_behind(right, ALL, 1)
        above = from_behind(left, ALL, -1)
        if sweep == 0:
            basis_b, basis_a = below[:, 256:], above[:, 256:]
        got = exchange(stage, ("z", "c"))
        if sweep == 0:
            tz = got[0::2, 64:, :] + got[1::2, 64:, :]
        sent = pl.pallas_call(
            spread_kernel,
            out_shape=hbm_out((16, 64, 128)),
            in_specs=[SMEM, VMEM, HBM, HBM, HBM],
            out_specs=HBM,
            scratch_shapes=[
                pltpu.VMEM((8, 64, 128), bf16), pltpu.VMEM((8, 256, 128), bf16),
                pltpu.VMEM((16, 64, 128), bf16), pltpu.VMEM((16, 64, 128), f32),
                pltpu.VMEM((16, 64, 128), bf16), DMAS((4,)),
            ],
            compiler_params=LIMIT,
            cost_estimate=pl.CostEstimate(
                flops=120_000_000, bytes_accessed=1_500_000, transcendentals=0
            ),
        )(place, *in_vmem(got), *in_hbm(tz, wd, wm))
        base, pre = pl.pallas_call(
            near_kernel,
            out_shape=(vmem_out((8, 256, 128), f32), vmem_out((8, 64, 128), f32)),
            in_specs=[SMEM] * 2 + [VMEM] * 3 + [HBM] * 9,
            out_specs=[VMEM, VMEM],
            scratch_shapes=[
                pltpu.VMEM((8, 6, 256, 256), bf16), pltpu.VMEM((8, 256, 128), f32),
                pltpu.VMEM((8, 2, 128), f32), pltpu.VMEM((8, 4, 64, 64), bf16),
                pltpu.VMEM((20, 256, 128), bf16), pltpu.VMEM((12, 128, 128), bf16),
                pltpu.VMEM((20, 64, 128), bf16), DMAS((9,)), DMAS((2, 8)),
            ],
            compiler_params=LIMIT,
            cost_estimate=pl.CostEstimate(
                flops=900_000_000, bytes_accessed=12_000_000, transcendentals=0
            ),
        )(
            near_local, far_local, *in_vmem(below, above, x),
            *in_hbm(
                near_tiles, rhs, noise, leaf_coupling, right, left, basis_b, basis_a, coef
            ),
        )
        fields = exchange(sent, ("x", "y"))
        if sweep < ITERS - 1:
            x, right, left, coef, stage = pl.pallas_call(
                update_kernel,
                out_shape=(
                    vmem_out((8, 256, 128), f32), hbm_out((SPAN, 256, 128)),
                    hbm_out((SPAN, 256, 128)), hbm_out((8, 64, 128)), hbm_out((16, 64, 128)),
                ),
                in_specs=[VMEM] * 3 + [HBM] * 4,
                out_specs=[VMEM] + [HBM] * 4,
                scratch_shapes=LOADED + [
                    pltpu.VMEM((8, 64, 256), bf16), pltpu.VMEM((64, 512), bf16),
                    pltpu.VMEM((8, 256, 128), bf16), pltpu.VMEM((8, 64, 128), bf16),
                    pltpu.VMEM((64, 128), bf16), DMAS((4,)), DMAS((21,)),
                ],
                compiler_params=LIMIT,
                cost_estimate=pl.CostEstimate(
                    flops=90_000_000, bytes_accessed=5_000_000, transcendentals=0
                ),
            )(
                *in_vmem(fields, base, pre), *in_hbm(basis_t, ltrans_t, leaf_basis, ltrans)
            )
        else:
            x = pl.pallas_call(
                last_kernel,
                out_shape=hbm_out((8, 256, 128), f32),
                in_specs=[VMEM] * 3 + [HBM] * 2,
                out_specs=HBM,
                scratch_shapes=[pltpu.VMEM((8, 256, 128), f32)] + LOADED + [DMAS((2,)), DMAS((4,))],
                compiler_params=LIMIT,
                cost_estimate=pl.CostEstimate(
                    flops=45_000_000, bytes_accessed=3_000_000, transcendentals=0
                ),
            )(*in_vmem(fields, base, pre), *in_hbm(basis_t, ltrans_t))
    return x.reshape(2048, 128)


def solution(mesh):
    finer = Mesh(mesh.devices.reshape(NX, NZ, NC, NY), ALL)
    spec = lambda n: P(ALL, *([None] * (n - 1)))
    return jax.shard_map(
        per_device,
        mesh=finer,
        in_specs=(
            spec(2), spec(1), spec(4), spec(2), spec(3), spec(3), spec(4), spec(2), spec(3),
            spec(4), spec(2), P("y", None, None, None), P("y", None),
        ),
        out_specs=P(ALL, None),
        check_vma=False,
    )
```

```python
import functools

import jax
import jax.numpy as jnp
from jax import lax
from jax.experimental import pallas as pl
from jax.experimental.pallas import tpu as pltpu
from jax.sharding import Mesh
from jax.sharding import PartitionSpec as P

SPAN = 6
ITERS = 4
NX, NZ, NC, NY = 4, 8, 2, 4
ALL = ("x", "z", "c", "y")
relax_step = 0.3
bf16, f32, i32 = jnp.bfloat16, jnp.float32, jnp.int32


def from_behind(value, axis, steps):
    count = lax.axis_size(axis)
    pairs = [(source, (source + steps) % count) for source in range(count)]
    return lax.ppermute(value, axis, pairs)


def exchange(chunks, axes):
    return lax.all_to_all(chunks, axes, split_axis=0, concat_axis=0, tiled=True)


def dot(a, b):
    return jnp.dot(a, b, preferred_element_type=f32)


def dot_t(a, b):
    return lax.dot_general(a, b, (((0,), (0,)), ((), ())), preferred_element_type=f32)


def whole(*dims):
    return pl.BlockSpec(dims, lambda *_: (0,) * len(dims))


VMEM = pl.BlockSpec(memory_space=pltpu.VMEM)
HBM = pl.BlockSpec(memory_space=pltpu.HBM)


def in_hbm(*arrays):
    return [pltpu.with_memory_space_constraint(a, pltpu.HBM) for a in arrays]


def in_vmem(*arrays):
    return [pltpu.with_memory_space_constraint(a, pltpu.VMEM) for a in arrays]


def hbm_out(dims, kind=bf16):
    return pltpu.HBM(dims, kind)


def vmem_out(dims, kind=bf16):
    return pltpu.VMEM(dims, kind)


def place(name):
    return lax.axis_index(name).astype(i32)


def setup_kernel(far_ref, mids_ref, transfer_ref, coupling_ref, mid_hbm, out_hbm, mid, out, sems):
    own = place("x") * 2 + place("z") // 4
    load = pltpu.make_async_copy(mid_hbm.at[own], mid, sems.at[0])
    load.start()
    lane = lax.broadcasted_iota(i32, (64, 128), 1)
    c = [coupling_ref[0, k].astype(f32) for k in range(4)]
    codes = jnp.zeros((64, 128), f32)
    for i in range(7):
        code = far_ref[0, i] // NY if i < 4 else mids_ref[own, i - 4]
        codes = jnp.where(lane == 64 + i, code.astype(f32), codes)
    t = transfer_ref[0]
    load.wait()
    folded = [dot_t(t, mid[k]) for k in range(3)]
    slots = [
        jnp.concatenate([c[0], c[1]], 1),
        jnp.concatenate([c[2], c[3]], 1),
        jnp.concatenate([folded[0], folded[1]], 1),
        jnp.where(lane < 64, jnp.concatenate([folded[2], folded[2]], 1), codes),
    ]
    for i in range(4):
        out[i] = slots[i].astype(bf16)
    outs = [pltpu.make_async_copy(out, out_hbm.at[q], sems.at[1 + q]) for q in range(NX * NY)]
    for o in outs:
        o.start()
    for o in outs:
        o.wait()


def weights_kernel(index_ref, got_ref, wd_ref, wm_ref):
    lane = lax.broadcasted_iota(i32, (64, 128), 1)
    x, y = place("x"), place("y")
    wd_ref[...] = jnp.zeros_like(wd_ref)
    wm_ref[...] = jnp.zeros_like(wm_ref)

    def half(value, source, target):
        swapped = jnp.concatenate([value[:, 64:], value[:, :64]], 1)
        moved = jnp.where(target == source, value, swapped)
        return jnp.where(lane // 64 == target, moved, 0.0)

    for xd in range(NX):
        q = xd * NY + y
        for k in range(4):
            sub = index_ref[q * 8 + k]

            @pl.when(sub // (NZ * NC) == x)
            def _(sub=sub, q=q, k=k, xd=xd):
                zf = lax.rem(sub // NC, NZ)
                value = half(got_ref[q, k // 2].astype(f32), k % 2, lax.rem(sub, NC))
                rows = pl.ds(xd * 64, 64)
                wd_ref[zf, rows, :] = (wd_ref[zf, rows, :].astype(f32) + value).astype(bf16)

    def mids(q, carry):
        for k in range(3):
            m = index_ref[q * 8 + 4 + k]

            @pl.when(m // 2 == y * NX + x)
            def _(m=m, k=k):
                value = half(got_ref[q, 2 + k // 2].astype(f32), k % 2, lax.rem(m, 2))
                wm_ref[q] = (wm_ref[q].astype(f32) + value).astype(bf16)

        return carry

    lax.fori_loop(0, NX * NY, mids, 0)


def coefficients(rounded, l, basis_ref, ltrans_ref, coef_ref):
    coef = dot(basis_ref[l], rounded).astype(bf16)
    coef_ref[l] = coef
    return dot(ltrans_ref[l], coef)


def first_kernel(
    rhs_ref, basis_ref, ltrans_ref, dtrans_ref,
    right_ref, left_ref, coef_ref, stage_hbm, basis_t_ref, ltrans_t_ref, ltrans_out_ref, dev, sems,
):
    total = jnp.zeros((64, 128), f32)
    for l in range(8):
        rounded = (relax_step * rhs_ref[l]).astype(bf16)
        halves = (basis_ref[l, :, :128], basis_ref[l, :, 128:])
        for ref, at in ((right_ref, l - 2), (left_ref, l)):
            if 0 <= at < SPAN:
                ref[at, 0:256, :] = rounded
                ref[at, 256:320, :] = halves[0]
                ref[at, 320:384, :] = halves[1]
        total = total + coefficients(rounded, l, basis_ref, ltrans_ref, coef_ref)
    t = dtrans_ref[0]
    dev[0:64, :] = total.astype(bf16)
    dev[64:96, :] = jnp.concatenate([t[:32, :], t[32:, :]], 1)
    outs = [pltpu.make_async_copy(dev, stage_hbm.at[j], sems.at[j]) for j in range(NZ * NC)]
    for o in outs:
        o.start()
    for i in range(4):
        basis_t_ref[i] = jnp.concatenate([basis_ref[2 * i], basis_ref[2 * i + 1]], 0).T
        pair = jnp.concatenate([ltrans_ref[2 * i], ltrans_ref[2 * i + 1]], 1)
        ltrans_t_ref[128 * i : 128 * i + 128, :] = pair.T
        ltrans_out_ref[:, 128 * i : 128 * i + 128] = pair
    for o in outs:
        o.wait()


def copies_of(pairs, sems):
    made = [pltpu.make_async_copy(a, b, sems.at[i]) for i, (a, b) in enumerate(pairs)]
    for c in made:
        c.start()
    return made


def spread_kernel(first, got, *refs):
    if first:
        wd_hbm, wm_hbm, out_hbm, tz_hbm, tz, wd, wm, total, out, sems = refs
        loads = [(wd_hbm, wd), (wm_hbm, wm)]
    else:
        tz_hbm, wd_hbm, wm_hbm, out_hbm, tz, wd, wm, total, out, sems = refs
        loads = [(wd_hbm, wd), (wm_hbm, wm), (tz_hbm, tz)]
    copies = copies_of(loads, sems)
    if first:
        for z in range(NZ):
            t = [got[2 * z + c, 64:96, :].astype(f32) for c in range(2)]
            t = [jnp.concatenate([v[:, :64], v[:, 64:]], 0) for v in t]
            tz[z] = jnp.concatenate(t, 1).astype(bf16)
        copies.append(pltpu.make_async_copy(tz, tz_hbm, sems.at[4]))
        copies[2].start()
    copies[0].wait()
    if not first:
        copies[2].wait()
    halves, dev = [], None
    for zh in range(2):
        mid = None
        for z in range(4 * zh, 4 * zh + 4):
            g = jnp.concatenate([got[2 * z, 0:64, :], got[2 * z + 1, 0:64, :]], 0)
            part = dot(tz[z], g)
            mid = part if mid is None else mid + part
            part = dot(wd[z], g)
            dev = part if dev is None else dev + part
        halves.append(mid.astype(bf16))
    copies[1].wait()
    value = dot(wm[...].reshape(1024, 128), jnp.concatenate(halves, 0)).reshape(16, 64, 128)
    total[...] = value
    out[...] = value.astype(bf16)
    y = place("y")
    for xd in range(NX):
        q = xd * NY + y
        out[q] = (total[q] + dev[xd * 64 : xd * 64 + 64, :]).astype(bf16)
    c = pltpu.make_async_copy(out, out_hbm, sems.at[3])
    c.start()
    if first:
        copies[2].wait()
    c.wait()


def near_kernel(first, near_ref, far_ref, below_ref, above_ref, *refs):
    if first:
        (tiles_hbm, rhs_hbm, noise_hbm, coupling_hbm, right_hbm, left_hbm, coef_hbm,
         base_ref, pre_ref, basis_hbm,
         tiles, rhs, noise, coupling, window, basis, wcoef, sems, leaf_sems) = refs
    else:
        (x_ref, tiles_hbm, rhs_hbm, noise_hbm, coupling_hbm, right_hbm, left_hbm, coef_hbm,
         basis_hbm, base_ref, pre_ref,
         tiles, rhs, noise, coupling, window, basis, wcoef, sems, leaf_sems) = refs
    vec, tail = pl.ds(0, 256), pl.ds(256, 128)
    device = ((place("x") * NZ + place("z")) * NC + place("c")) * NY + place("y")
    offset = 2048 + SPAN - device * 8

    def local(index):
        return lax.rem(index + offset, 2048)

    pairs = [
        (below_ref.at[:, vec, :], window.at[0:SPAN]),
        (left_hbm.at[:, vec, :], window.at[SPAN : 2 * SPAN]),
        (right_hbm.at[SPAN - 2 : SPAN, vec, :], window.at[2 * SPAN : SPAN + 8]),
        (above_ref.at[:, vec, :], window.at[SPAN + 8 : 2 * SPAN + 8]),
        (coef_hbm, wcoef.at[SPAN : SPAN + 8]),
        (noise_hbm, noise),
        (coupling_hbm, coupling),
    ]
    if first:
        pairs.append((below_ref.at[:, tail, :], basis.at[0:SPAN]))
        pairs.append((above_ref.at[:, tail, :], basis.at[SPAN : 2 * SPAN]))
    else:
        pairs.append((basis_hbm, basis))
    copies = copies_of(pairs, sems)

    def leaf_copies(l):
        pairs = ((tiles_hbm, tiles), (rhs_hbm, rhs))
        return [pltpu.make_async_copy(a.at[l], b.at[l], leaf_sems.at[i, l]) for i, (a, b) in enumerate(pairs)]

    for l in range(DEPTH):
        for c in leaf_copies(l):
            c.start()
    for c in copies:
        c.wait()
    if first:
        kept = pltpu.make_async_copy(basis, basis_hbm, sems.at[9])
        kept.start()
    for i in range(2 * SPAN):
        at = i if i < SPAN else i + 8
        v, b = window[at], basis[i]
        wcoef[at] = (dot(b[0:64, :], v[:128]) + dot(b[64:128, :], v[128:])).astype(bf16)
    for l in range(8):
        part = None
        for k in range(4):
            more = dot(coupling[l, k], wcoef[local(far_ref[l, k])])
            part = more if part is None else part + more
        pre_ref[l] = part
        if l + DEPTH < 8:
            for c in leaf_copies(l + DEPTH):
                c.start()
        for c in leaf_copies(l):
            c.wait()
        near = dot(
            jnp.concatenate([tiles[l, k] for k in range(6)], 1),
            jnp.concatenate([window[local(near_ref[l, k])] for k in range(6)], 0),
        )
        scale = noise[l]
        for h in range(2):
            rows = pl.ds(h * 128, 128)
            column = jnp.broadcast_to(scale[h : h + 1, :], (128, 128)).T
            side = rhs[l, rows, :]
            value = relax_step * side if first else x_ref[l, rows, :]
            image = near[h * 128 : h * 128 + 128, :] + column * value
            base_ref[l, rows, :] = value + relax_step * (side - image)
    if first:
        kept.wait()


def corrected(got, base, pre, basis_t_hbm, ltrans_t_hbm, basis_t, ltrans_t, sems, more):
    pairs = [(ltrans_t_hbm, ltrans_t), (basis_t_hbm, basis_t)] + more
    copies = copies_of(pairs, sems)
    total = got[0].astype(f32)
    for q in range(1, NX * NY):
        total = total + got[q].astype(f32)
    for c in copies:
        c.wait()
    leaf = (pre[...].reshape(512, 128) + dot(ltrans_t[...], total.astype(bf16))).astype(bf16)
    zero = jnp.zeros((64, 128), bf16)
    for l in range(8):
        own = leaf[64 * l : 64 * l + 64, :]
        pair = jnp.concatenate([own, zero] if l % 2 == 0 else [zero, own], 0)
        yield l, base[l] - relax_step * dot(basis_t[l // 2], pair)


def update_kernel(
    got, base, pre, basis_t_hbm, ltrans_t_hbm, basis_hbm, ltrans_hbm,
    x_ref, right_hbm, left_hbm, coef_hbm, stage_hbm,
    basis_t, ltrans_t, basis, ltrans, rounded, coef, dev, sems, out_sems,
):
    outs = []

    def send(a, b):
        c = pltpu.make_async_copy(a, b, out_sems.at[len(outs)])
        c.start()
        outs.append(c)

    values = corrected(
        got, base, pre, basis_t_hbm, ltrans_t_hbm, basis_t, ltrans_t, sems,
        [(basis_hbm, basis), (ltrans_hbm, ltrans)],
    )
    for l, value in values:
        x_ref[l] = value
        rounded[l] = value.astype(bf16)
        if l == 3:
            send(rounded.at[0:4], left_hbm.at[0:4])
            send(rounded.at[2:4], right_hbm.at[0:2])
    send(rounded.at[4:6], left_hbm.at[4:6])
    send(rounded.at[4:8], right_hbm.at[2:6])
    for l in range(8):
        coef[l] = dot(basis[l], rounded[l]).astype(bf16)
    dev[...] = dot(ltrans[...], coef[...].reshape(512, 128)).astype(bf16)
    for j in range(NZ * NC):
        send(dev, stage_hbm.at[j])
    send(coef, coef_hbm)
    for c in outs:
        c.wait()


def last_kernel(
    got, base, pre, basis_t_hbm, ltrans_t_hbm, x_hbm, x, basis_t, ltrans_t, sems, out_sems
):
    outs = []
    for l, value in corrected(got, base, pre, basis_t_hbm, ltrans_t_hbm, basis_t, ltrans_t, sems, []):
        x[l] = value
        if l % 2:
            pair = pl.ds(l - 1, 2)
            outs.append(pltpu.make_async_copy(x.at[pair], x_hbm.at[pair], out_sems.at[l // 2]))
            outs[-1].start()
    for c in outs:
        c.wait()


LOADED = [pltpu.VMEM((4, 256, 128), bf16), pltpu.VMEM((512, 64), bf16)]
DMAS = pltpu.SemaphoreType.DMA
DEPTH = 3


def shape(dims, kind=bf16):
    return jax.ShapeDtypeStruct(dims, kind)


LIMIT = pltpu.CompilerParams(vmem_limit_bytes=24 << 20)
SMEM = pl.BlockSpec(memory_space=pltpu.SMEM)


def per_device(
    right_side, noise_var, near_tiles, near_index, leaf_basis, leaf_transfer, leaf_coupling,
    far_leaf, dev_transfer, dev_coupling, far_dev, mid_coupling, far_mid,
):
    rhs = right_side.reshape(8, 256, 128)
    noise = noise_var.reshape(8, 2, 128)

    setup = pl.pallas_call(
        setup_kernel,
        out_shape=hbm_out((16, 4, 64, 128)),
        grid=(1,),
        in_specs=[SMEM, SMEM, whole(1, 64, 64), whole(1, 4, 64, 64), HBM],
        out_specs=HBM,
        scratch_shapes=[
            pltpu.VMEM((3, 64, 64), bf16), pltpu.VMEM((4, 64, 128), bf16), DMAS((17,))
        ],
        cost_estimate=pl.CostEstimate(flops=4_000_000, bytes_accessed=1_200_000, transcendentals=0),
    )(far_dev, far_mid, dev_transfer, dev_coupling, mid_coupling)

    right, left, coef, stage, basis_t, ltrans_t, ltrans = pl.pallas_call(
        first_kernel,
        out_shape=(
            shape((SPAN, 384, 128)), shape((SPAN, 384, 128)), shape((8, 64, 128)),
            hbm_out((16, 96, 128)), shape((4, 256, 128)), shape((512, 64)), shape((64, 512)),
        ),
        grid=(1,),
        in_specs=[whole(8, 256, 128), whole(8, 64, 256), whole(8, 64, 64), whole(1, 64, 64)],
        out_specs=[
            whole(SPAN, 384, 128), whole(SPAN, 384, 128), whole(8, 64, 128), HBM,
            whole(4, 256, 128), whole(512, 64), whole(64, 512),
        ],
        scratch_shapes=[pltpu.VMEM((96, 128), bf16), DMAS((16,))],
        cost_estimate=pl.CostEstimate(flops=42_000_000, bytes_accessed=4_500_000, transcendentals=0),
    )(rhs, leaf_basis, leaf_transfer, dev_transfer)

    got_setup = exchange(setup, ("x", "y"))
    weights_in = got_setup[:, 3, 0, 64:72].astype(f32).astype(i32).reshape(-1)
    wd, wm = pl.pallas_call(
        weights_kernel,
        out_shape=(shape((8, 256, 128)), shape((16, 64, 128))),
        grid=(1,),
        in_specs=[SMEM, whole(16, 4, 64, 128)],
        out_specs=[whole(8, 256, 128), whole(16, 64, 128)],
        cost_estimate=pl.CostEstimate(flops=1_000_000, bytes_accessed=2_000_000, transcendentals=0),
    )(weights_in, got_setup)

    basis = tz = x = None
    for sweep in range(ITERS):
        first = sweep == 0
        below = from_behind(right, ALL, 1)
        above = from_behind(left, ALL, -1)
        got = exchange(stage, ("z", "c"))
        tz_shape = hbm_out((8, 64, 128))
        result = pl.pallas_call(
            functools.partial(spread_kernel, first),
            out_shape=(hbm_out((16, 64, 128)),) + ((tz_shape,) if first else ()),
            in_specs=[VMEM] + [HBM] * (2 if first else 3),
            out_specs=(HBM,) * (2 if first else 1),
            scratch_shapes=[
                pltpu.VMEM((8, 64, 128), bf16), pltpu.VMEM((8, 256, 128), bf16),
                pltpu.VMEM((16, 64, 128), bf16), pltpu.VMEM((16, 64, 128), f32),
                pltpu.VMEM((16, 64, 128), bf16), DMAS((5,)),
            ],
            compiler_params=LIMIT,
            cost_estimate=pl.CostEstimate(
                flops=120_000_000, bytes_accessed=1_500_000, transcendentals=0
            ),
        )(*in_vmem(got), *in_hbm(*(() if first else (tz,)), wd, wm))
        sent = result[0]
        tz = result[1] if first else tz
        basis_shape = hbm_out((2 * SPAN, 128, 128))
        result = pl.pallas_call(
            functools.partial(near_kernel, first),
            out_shape=(vmem_out((8, 256, 128), f32), vmem_out((8, 64, 128), f32))
            + ((basis_shape,) if first else ()),
            in_specs=[SMEM] * 2 + [VMEM] * (2 if first else 3) + [HBM] * (7 if first else 8),
            out_specs=(VMEM, VMEM) + ((HBM,) if first else ()),
            scratch_shapes=[
                pltpu.VMEM((8, 6, 256, 256), bf16), pltpu.VMEM((8, 256, 128), f32),
                pltpu.VMEM((8, 2, 128), f32), pltpu.VMEM((8, 4, 64, 64), bf16),
                pltpu.VMEM((20, 256, 128), bf16), pltpu.VMEM((12, 128, 128), bf16),
                pltpu.VMEM((20, 64, 128), bf16), DMAS((10,)), DMAS((2, 8)),
            ],
            compiler_params=LIMIT,
            cost_estimate=pl.CostEstimate(
                flops=900_000_000, bytes_accessed=12_000_000, transcendentals=0
            ),
        )(
            near_index, far_leaf, *in_vmem(below, above, *(() if first else (x,))),
            *in_hbm(near_tiles, rhs, noise, leaf_coupling, right, left, coef),
            *(() if first else in_hbm(basis)),
        )
        base, pre = result[:2]
        basis = result[2] if first else basis
        fields = exchange(sent, ("x", "y"))
        if sweep < ITERS - 1:
            x, right, left, coef, stage = pl.pallas_call(
                update_kernel,
                out_shape=(
                    vmem_out((8, 256, 128), f32), hbm_out((SPAN, 256, 128)),
                    hbm_out((SPAN, 256, 128)), hbm_out((8, 64, 128)), hbm_out((16, 64, 128)),
                ),
                in_specs=[VMEM] * 3 + [HBM] * 4,
                out_specs=[VMEM] + [HBM] * 4,
                scratch_shapes=LOADED + [
                    pltpu.VMEM((8, 64, 256), bf16), pltpu.VMEM((64, 512), bf16),
                    pltpu.VMEM((8, 256, 128), bf16), pltpu.VMEM((8, 64, 128), bf16),
                    pltpu.VMEM((64, 128), bf16), DMAS((4,)), DMAS((21,)),
                ],
                compiler_params=LIMIT,
                cost_estimate=pl.CostEstimate(
                    flops=90_000_000, bytes_accessed=5_000_000, transcendentals=0
                ),
            )(
                *in_vmem(fields, base, pre), *in_hbm(basis_t, ltrans_t, leaf_basis, ltrans)
            )
        else:
            x = pl.pallas_call(
                last_kernel,
                out_shape=hbm_out((8, 256, 128), f32),
                in_specs=[VMEM] * 3 + [HBM] * 2,
                out_specs=HBM,
                scratch_shapes=[pltpu.VMEM((8, 256, 128), f32)] + LOADED + [DMAS((2,)), DMAS((4,))],
                compiler_params=LIMIT,
                cost_estimate=pl.CostEstimate(
                    flops=45_000_000, bytes_accessed=3_000_000, transcendentals=0
                ),
            )(*in_vmem(fields, base, pre), *in_hbm(basis_t, ltrans_t))
    return x.reshape(2048, 128)


def solution(mesh):
    finer = Mesh(mesh.devices.reshape(NX, NZ, NC, NY), ALL)
    spec = lambda n: P(ALL, *([None] * (n - 1)))
    return jax.shard_map(
        per_device,
        mesh=finer,
        in_specs=(
            spec(2), spec(1), spec(4), spec(2), spec(3), spec(3), spec(4), spec(2), spec(3),
            spec(4), spec(2), P("y", None, None, None), P("y", None),
        ),
        out_specs=P(ALL, None),
        check_vma=False,
    )
```

```python
import functools

import jax
import jax.numpy as jnp
from jax import lax
from jax.experimental import pallas as pl
from jax.experimental.pallas import tpu as pltpu
from jax.sharding import Mesh
from jax.sharding import PartitionSpec as P

SPAN = 6
ITERS = 4
NX, NZ, NC, NY = 4, 8, 2, 4
ALL = ("x", "z", "c", "y")
relax_step = 0.3
bf16, f32, i32 = jnp.bfloat16, jnp.float32, jnp.int32


def from_behind(value, axis, steps):
    count = lax.axis_size(axis)
    pairs = [(source, (source + steps) % count) for source in range(count)]
    return lax.ppermute(value, axis, pairs)


def exchange(chunks, axes):
    return lax.all_to_all(chunks, axes, split_axis=0, concat_axis=0, tiled=True)


def dot(a, b):
    return jnp.dot(a, b, preferred_element_type=f32)


def dot_t(a, b):
    return lax.dot_general(a, b, (((0,), (0,)), ((), ())), preferred_element_type=f32)


def whole(*dims):
    return pl.BlockSpec(dims, lambda *_: (0,) * len(dims))


VMEM = pl.BlockSpec(memory_space=pltpu.VMEM)
HBM = pl.BlockSpec(memory_space=pltpu.HBM)


def in_hbm(*arrays):
    return [pltpu.with_memory_space_constraint(a, pltpu.HBM) for a in arrays]


def in_vmem(*arrays):
    return [pltpu.with_memory_space_constraint(a, pltpu.VMEM) for a in arrays]


def hbm_out(dims, kind=bf16):
    return pltpu.HBM(dims, kind)


def vmem_out(dims, kind=bf16):
    return pltpu.VMEM(dims, kind)


def place(name):
    return lax.axis_index(name).astype(i32)


def setup_kernel(far_ref, mids_ref, transfer_ref, coupling_ref, mid_hbm, out_hbm, mid, out, sems):
    own = place("x") * 2 + place("z") // 4
    load = pltpu.make_async_copy(mid_hbm.at[own], mid, sems.at[0])
    load.start()
    lane = lax.broadcasted_iota(i32, (64, 128), 1)
    c = [coupling_ref[0, k].astype(f32) for k in range(4)]
    codes = jnp.zeros((64, 128), f32)
    for i in range(7):
        code = far_ref[0, i] // NY if i < 4 else mids_ref[i - 4, own]
        codes = jnp.where(lane == 64 + i, code.astype(f32), codes)
    t = transfer_ref[0]
    load.wait()
    folded = [dot_t(t, mid[k]) for k in range(3)]
    slots = [
        jnp.concatenate([c[0], c[1]], 1),
        jnp.concatenate([c[2], c[3]], 1),
        jnp.concatenate([folded[0], folded[1]], 1),
        jnp.where(lane < 64, jnp.concatenate([folded[2], folded[2]], 1), codes),
    ]
    for i in range(4):
        out[i] = slots[i].astype(bf16)
    outs = [pltpu.make_async_copy(out, out_hbm.at[q], sems.at[1 + q]) for q in range(NX * NY)]
    for o in outs:
        o.start()
    for o in outs:
        o.wait()


def weights_kernel(index_ref, got_ref, wd_ref, wm_ref):
    lane = lax.broadcasted_iota(i32, (64, 128), 1)
    x, y = place("x"), place("y")
    wd_ref[...] = jnp.zeros_like(wd_ref)
    wm_ref[...] = jnp.zeros_like(wm_ref)

    def half(value, source, target):
        swapped = jnp.concatenate([value[:, 64:], value[:, :64]], 1)
        moved = jnp.where(target == source, value, swapped)
        return jnp.where(lane // 64 == target, moved, 0.0)

    for xd in range(NX):
        q = xd * NY + y
        for k in range(4):
            sub = index_ref[q * 8 + k]

            @pl.when(sub // (NZ * NC) == x)
            def _(sub=sub, q=q, k=k, xd=xd):
                zf = lax.rem(sub // NC, NZ)
                value = half(got_ref[q, k // 2].astype(f32), k % 2, lax.rem(sub, NC))
                rows = pl.ds(xd * 64, 64)
                wd_ref[zf, rows, :] = (wd_ref[zf, rows, :].astype(f32) + value).astype(bf16)

    def mids(q, carry):
        for k in range(3):
            m = index_ref[q * 8 + 4 + k]

            @pl.when(m // 2 == y * NX + x)
            def _(m=m, k=k):
                value = half(got_ref[q, 2 + k // 2].astype(f32), k % 2, lax.rem(m, 2))
                wm_ref[q] = (wm_ref[q].astype(f32) + value).astype(bf16)

        return carry

    lax.fori_loop(0, NX * NY, mids, 0)


def coefficients(rounded, l, basis_ref, ltrans_ref, coef_ref):
    coef = dot(basis_ref[l], rounded).astype(bf16)
    coef_ref[l] = coef
    return dot(ltrans_ref[l], coef)


def first_kernel(
    rhs_ref, basis_ref, ltrans_ref, dtrans_ref,
    right_ref, left_ref, coef_ref, stage_hbm, basis_t_ref, ltrans_t_ref, ltrans_out_ref, dev, sems,
):
    total = jnp.zeros((64, 128), f32)
    for l in range(8):
        rounded = (relax_step * rhs_ref[l]).astype(bf16)
        halves = (basis_ref[l, :, :128], basis_ref[l, :, 128:])
        for ref, at in ((right_ref, l - 2), (left_ref, l)):
            if 0 <= at < SPAN:
                ref[at, 0:256, :] = rounded
                ref[at, 256:320, :] = halves[0]
                ref[at, 320:384, :] = halves[1]
        total = total + coefficients(rounded, l, basis_ref, ltrans_ref, coef_ref)
    t = dtrans_ref[0]
    dev[0:64, :] = total.astype(bf16)
    dev[64:96, :] = jnp.concatenate([t[:32, :], t[32:, :]], 1)
    outs = [pltpu.make_async_copy(dev, stage_hbm.at[j], sems.at[j]) for j in range(NZ * NC)]
    for o in outs:
        o.start()
    for i in range(4):
        basis_t_ref[i] = jnp.concatenate([basis_ref[2 * i], basis_ref[2 * i + 1]], 0).T
        pair = jnp.concatenate([ltrans_ref[2 * i], ltrans_ref[2 * i + 1]], 1)
        ltrans_t_ref[128 * i : 128 * i + 128, :] = pair.T
        ltrans_out_ref[:, 128 * i : 128 * i + 128] = pair
    for o in outs:
        o.wait()


def copies_of(pairs, sems):
    made = [pltpu.make_async_copy(a, b, sems.at[i]) for i, (a, b) in enumerate(pairs)]
    for c in made:
        c.start()
    return made


def spread_kernel(first, got, *refs):
    if first:
        wd_hbm, wm_hbm, out_hbm, tz_hbm, tz, wd, wm, total, out, sems = refs
        loads = [(wd_hbm, wd), (wm_hbm, wm)]
    else:
        tz_hbm, wd_hbm, wm_hbm, out_hbm, tz, wd, wm, total, out, sems = refs
        loads = [(wd_hbm, wd), (wm_hbm, wm), (tz_hbm, tz)]
    copies = copies_of(loads, sems)
    if first:
        for z in range(NZ):
            t = [got[2 * z + c, 64:96, :].astype(f32) for c in range(2)]
            t = [jnp.concatenate([v[:, :64], v[:, 64:]], 0) for v in t]
            tz[z] = jnp.concatenate(t, 1).astype(bf16)
        copies.append(pltpu.make_async_copy(tz, tz_hbm, sems.at[4]))
        copies[2].start()
    copies[0].wait()
    if not first:
        copies[2].wait()
    halves, dev = [], None
    for zh in range(2):
        mid = None
        for z in range(4 * zh, 4 * zh + 4):
            g = jnp.concatenate([got[2 * z, 0:64, :], got[2 * z + 1, 0:64, :]], 0)
            part = dot(tz[z], g)
            mid = part if mid is None else mid + part
            part = dot(wd[z], g)
            dev = part if dev is None else dev + part
        halves.append(mid.astype(bf16))
    copies[1].wait()
    value = dot(wm[...].reshape(1024, 128), jnp.concatenate(halves, 0)).reshape(16, 64, 128)
    total[...] = value
    out[...] = value.astype(bf16)
    y = place("y")
    for xd in range(NX):
        q = xd * NY + y
        out[q] = (total[q] + dev[xd * 64 : xd * 64 + 64, :]).astype(bf16)
    c = pltpu.make_async_copy(out, out_hbm, sems.at[3])
    c.start()
    if first:
        copies[2].wait()
    c.wait()


def near_kernel(first, near_ref, far_ref, below_ref, above_ref, *refs):
    if first:
        (tiles_hbm, rhs_hbm, noise_hbm, coupling_hbm, right_hbm, left_hbm, coef_hbm,
         base_ref, pre_ref, basis_hbm,
         tiles, rhs, noise, coupling, window, basis, wcoef, sems, leaf_sems) = refs
    else:
        (x_ref, right_hbm, left_hbm, coef_hbm, tiles_hbm, rhs_hbm, noise_hbm, coupling_hbm,
         basis_hbm, base_ref, pre_ref,
         tiles, rhs, noise, coupling, window, basis, wcoef, sems, leaf_sems) = refs
    vec, tail = pl.ds(0, 256), pl.ds(256, 128)
    device = ((place("x") * NZ + place("z")) * NC + place("c")) * NY + place("y")
    offset = 2048 + SPAN - device * 8

    def local(index):
        return lax.rem(index + offset, 2048)

    pairs = [
        (below_ref.at[:, vec, :], window.at[0:SPAN]),
        (left_hbm.at[:, vec, :], window.at[SPAN : 2 * SPAN]),
        (right_hbm.at[SPAN - 2 : SPAN, vec, :], window.at[2 * SPAN : SPAN + 8]),
        (above_ref.at[:, vec, :], window.at[SPAN + 8 : 2 * SPAN + 8]),
        (noise_hbm, noise),
    ]
    later = [(coef_hbm, wcoef.at[SPAN : SPAN + 8]), (coupling_hbm, coupling)]
    if first:
        later.append((below_ref.at[:, tail, :], basis.at[0:SPAN]))
        later.append((above_ref.at[:, tail, :], basis.at[SPAN : 2 * SPAN]))
    else:
        later.append((basis_hbm, basis))
    copies = copies_of(pairs, sems)

    def leaf_copies(l):
        pairs = ((tiles_hbm, tiles), (rhs_hbm, rhs))
        return [pltpu.make_async_copy(a.at[l], b.at[l], leaf_sems.at[i, l]) for i, (a, b) in enumerate(pairs)]

    for l in range(DEPTH):
        for c in leaf_copies(l):
            c.start()
    late = [pltpu.make_async_copy(p, q, sems.at[5 + i]) for i, (p, q) in enumerate(later)]
    for c in late:
        c.start()
    for c in copies:
        c.wait()

    def coefficient_part():
        for c in late:
            c.wait()
        for i in range(2 * SPAN):
            at = i if i < SPAN else i + 8
            v, b = window[at], basis[i]
            wcoef[at] = (dot(b[0:64, :], v[:128]) + dot(b[64:128, :], v[128:])).astype(bf16)
        for l in range(8):
            part = None
            for k in range(4):
                more = dot(coupling[l, k], wcoef[local(far_ref[k, l])])
                part = more if part is None else part + more
            pre_ref[l] = part

    for l in range(8):
        if l + DEPTH < 8:
            for c in leaf_copies(l + DEPTH):
                c.start()
        for c in leaf_copies(l):
            c.wait()
        near = dot(
            jnp.concatenate([tiles[l, k] for k in range(6)], 1),
            jnp.concatenate([window[local(near_ref[l, k])] for k in range(6)], 0),
        )
        scale = noise[l]
        for h in range(2):
            rows = pl.ds(h * 128, 128)
            column = jnp.broadcast_to(scale[h : h + 1, :], (128, 128)).T
            side = rhs[l, rows, :]
            value = relax_step * side if first else x_ref[l, rows, :]
            image = near[h * 128 : h * 128 + 128, :] + column * value
            base_ref[l, rows, :] = value + relax_step * (side - image)
        if l == 3:
            coefficient_part()
            if first:
                kept = pltpu.make_async_copy(basis, basis_hbm, sems.at[9])
                kept.start()
    if first:
        kept.wait()


def corrected(got, base, pre, basis_t_hbm, ltrans_t_hbm, basis_t, ltrans_t, sems, more):
    pairs = [(ltrans_t_hbm, ltrans_t), (basis_t_hbm, basis_t)] + more
    copies = copies_of(pairs, sems)
    total = got[0].astype(f32)
    for q in range(1, NX * NY):
        total = total + got[q].astype(f32)
    for c in copies:
        c.wait()
    leaf = (pre[...].reshape(512, 128) + dot(ltrans_t[...], total.astype(bf16))).astype(bf16)
    zero = jnp.zeros((64, 128), bf16)
    for l in range(8):
        own = leaf[64 * l : 64 * l + 64, :]
        pair = jnp.concatenate([own, zero] if l % 2 == 0 else [zero, own], 0)
        yield l, base[l] - relax_step * dot(basis_t[l // 2], pair)


def update_kernel(
    got, base, pre, basis_t_hbm, ltrans_t_hbm, basis_hbm, ltrans_hbm,
    x_ref, right_ref, left_ref, coef_ref, stage_hbm, basis_t, ltrans_t, basis, ltrans, dev, sems,
    out_sems,
):
    values = corrected(
        got, base, pre, basis_t_hbm, ltrans_t_hbm, basis_t, ltrans_t, sems,
        [(basis_hbm, basis), (ltrans_hbm, ltrans)],
    )
    for l, value in values:
        x_ref[l] = value
        rounded = value.astype(bf16)
        if l >= 2:
            right_ref[l - 2] = rounded
        if l < SPAN:
            left_ref[l] = rounded
    for l in range(8):
        rounded = left_ref[l] if l < SPAN else right_ref[l - 2]
        coef_ref[l] = dot(basis[l], rounded).astype(bf16)
    dev[...] = dot(ltrans[...], coef_ref[...].reshape(512, 128)).astype(bf16)
    outs = [pltpu.make_async_copy(dev, stage_hbm.at[j], out_sems.at[j]) for j in range(NZ * NC)]
    for c in outs:
        c.start()
    for c in outs:
        c.wait()


def last_kernel(
    got, base, pre, basis_t_hbm, ltrans_t_hbm, x_hbm, x, basis_t, ltrans_t, sems, out_sems
):
    outs = []
    for l, value in corrected(got, base, pre, basis_t_hbm, ltrans_t_hbm, basis_t, ltrans_t, sems, []):
        x[l] = value
        if l % 2:
            pair = pl.ds(l - 1, 2)
            outs.append(pltpu.make_async_copy(x.at[pair], x_hbm.at[pair], out_sems.at[l // 2]))
            outs[-1].start()
    for c in outs:
        c.wait()


LOADED = [pltpu.VMEM((4, 256, 128), bf16), pltpu.VMEM((512, 64), bf16)]
DMAS = pltpu.SemaphoreType.DMA
DEPTH = 3


def shape(dims, kind=bf16):
    return jax.ShapeDtypeStruct(dims, kind)


LIMIT = pltpu.CompilerParams(vmem_limit_bytes=24 << 20)
SMEM = pl.BlockSpec(memory_space=pltpu.SMEM)


def per_device(
    right_side, noise_var, near_tiles, near_index, leaf_basis, leaf_transfer, leaf_coupling,
    far_leaf, dev_transfer, dev_coupling, far_dev, mid_coupling, far_mid,
):
    rhs = right_side.reshape(8, 256, 128)
    noise = noise_var.reshape(8, 2, 128)

    setup = pl.pallas_call(
        setup_kernel,
        out_shape=hbm_out((16, 4, 64, 128)),
        grid=(1,),
        in_specs=[SMEM, SMEM, whole(1, 64, 64), whole(1, 4, 64, 64), HBM],
        out_specs=HBM,
        scratch_shapes=[
            pltpu.VMEM((3, 64, 64), bf16), pltpu.VMEM((4, 64, 128), bf16), DMAS((17,))
        ],
        cost_estimate=pl.CostEstimate(flops=4_000_000, bytes_accessed=1_200_000, transcendentals=0),
    )(far_dev, far_mid.T, dev_transfer, dev_coupling, mid_coupling)

    right, left, coef, stage, basis_t, ltrans_t, ltrans = pl.pallas_call(
        first_kernel,
        out_shape=(
            shape((SPAN, 384, 128)), shape((SPAN, 384, 128)), shape((8, 64, 128)),
            hbm_out((16, 96, 128)), shape((4, 256, 128)), shape((512, 64)), shape((64, 512)),
        ),
        grid=(1,),
        in_specs=[whole(8, 256, 128), whole(8, 64, 256), whole(8, 64, 64), whole(1, 64, 64)],
        out_specs=[
            whole(SPAN, 384, 128), whole(SPAN, 384, 128), whole(8, 64, 128), HBM,
            whole(4, 256, 128), whole(512, 64), whole(64, 512),
        ],
        scratch_shapes=[pltpu.VMEM((96, 128), bf16), DMAS((16,))],
        cost_estimate=pl.CostEstimate(flops=42_000_000, bytes_accessed=4_500_000, transcendentals=0),
    )(rhs, leaf_basis, leaf_transfer, dev_transfer)

    got_setup = exchange(setup, ("x", "y"))
    weights_in = got_setup[:, 3, 0, 64:72].astype(f32).astype(i32).reshape(-1)
    wd, wm = pl.pallas_call(
        weights_kernel,
        out_shape=(shape((8, 256, 128)), shape((16, 64, 128))),
        grid=(1,),
        in_specs=[SMEM, whole(16, 4, 64, 128)],
        out_specs=[whole(8, 256, 128), whole(16, 64, 128)],
        cost_estimate=pl.CostEstimate(flops=1_000_000, bytes_accessed=2_000_000, transcendentals=0),
    )(weights_in, got_setup)

    basis = tz = x = None
    for sweep in range(ITERS):
        first = sweep == 0
        below = from_behind(right, ALL, 1)
        above = from_behind(left, ALL, -1)
        got = exchange(stage, ("z", "c"))
        tz_shape = hbm_out((8, 64, 128))
        result = pl.pallas_call(
            functools.partial(spread_kernel, first),
            out_shape=(hbm_out((16, 64, 128)),) + ((tz_shape,) if first else ()),
            in_specs=[VMEM] + [HBM] * (2 if first else 3),
            out_specs=(HBM,) * (2 if first else 1),
            scratch_shapes=[
                pltpu.VMEM((8, 64, 128), bf16), pltpu.VMEM((8, 256, 128), bf16),
                pltpu.VMEM((16, 64, 128), bf16), pltpu.VMEM((16, 64, 128), f32),
                pltpu.VMEM((16, 64, 128), bf16), DMAS((5,)),
            ],
            compiler_params=LIMIT,
            cost_estimate=pl.CostEstimate(
                flops=120_000_000, bytes_accessed=1_500_000, transcendentals=0
            ),
        )(*in_vmem(got), *in_hbm(*(() if first else (tz,)), wd, wm))
        sent = result[0]
        tz = result[1] if first else tz
        basis_shape = hbm_out((2 * SPAN, 128, 128))
        result = pl.pallas_call(
            functools.partial(near_kernel, first),
            out_shape=(vmem_out((8, 256, 128), f32), vmem_out((8, 64, 128), f32))
            + ((basis_shape,) if first else ()),
            in_specs=[SMEM] * 2 + [VMEM] * (2 if first else 6) + [HBM] * (7 if first else 5),
            input_output_aliases={} if first else {4: 0},
            out_specs=(VMEM, VMEM) + ((HBM,) if first else ()),
            scratch_shapes=[
                pltpu.VMEM((8, 6, 256, 256), bf16), pltpu.VMEM((8, 256, 128), f32),
                pltpu.VMEM((8, 2, 128), f32), pltpu.VMEM((8, 4, 64, 64), bf16),
                pltpu.VMEM((20, 256, 128), bf16), pltpu.VMEM((12, 128, 128), bf16),
                pltpu.VMEM((20, 64, 128), bf16), DMAS((10,)), DMAS((2, 8)),
            ],
            compiler_params=LIMIT,
            cost_estimate=pl.CostEstimate(
                flops=900_000_000, bytes_accessed=12_000_000, transcendentals=0
            ),
        )(
            near_index, far_leaf.T,
            *in_vmem(below, above, *(() if first else (x, right, left, coef))),
            *in_hbm(near_tiles, rhs, noise, leaf_coupling),
            *in_hbm(*((right, left, coef) if first else (basis,))),
        )
        base, pre = result[:2]
        basis = result[2] if first else basis
        fields = exchange(sent, ("x", "y"))
        if sweep < ITERS - 1:
            x, right, left, coef, stage = pl.pallas_call(
                update_kernel,
                out_shape=(
                    vmem_out((8, 256, 128), f32), vmem_out((SPAN, 256, 128)),
                    vmem_out((SPAN, 256, 128)), vmem_out((8, 64, 128)), hbm_out((16, 64, 128)),
                ),
                in_specs=[VMEM] * 3 + [HBM] * 4,
                out_specs=[VMEM] * 4 + [HBM],
                scratch_shapes=LOADED + [
                    pltpu.VMEM((8, 64, 256), bf16), pltpu.VMEM((64, 512), bf16),
                    pltpu.VMEM((64, 128), bf16), DMAS((4,)), DMAS((16,)),
                ],
                compiler_params=LIMIT,
                cost_estimate=pl.CostEstimate(
                    flops=90_000_000, bytes_accessed=5_000_000, transcendentals=0
                ),
            )(
                *in_vmem(fields, base, pre), *in_hbm(basis_t, ltrans_t, leaf_basis, ltrans)
            )
        else:
            x = pl.pallas_call(
                last_kernel,
                out_shape=hbm_out((8, 256, 128), f32),
                in_specs=[VMEM] * 3 + [HBM] * 2,
                out_specs=HBM,
                scratch_shapes=[pltpu.VMEM((8, 256, 128), f32)] + LOADED + [DMAS((2,)), DMAS((4,))],
                compiler_params=LIMIT,
                cost_estimate=pl.CostEstimate(
                    flops=45_000_000, bytes_accessed=3_000_000, transcendentals=0
                ),
            )(*in_vmem(fields, base, pre), *in_hbm(basis_t, ltrans_t))
    return x.reshape(2048, 128)


def solution(mesh):
    finer = Mesh(mesh.devices.reshape(NX, NZ, NC, NY), ALL)
    spec = lambda n: P(ALL, *([None] * (n - 1)))
    return jax.shard_map(
        per_device,
        mesh=finer,
        in_specs=(
            spec(2), spec(1), spec(4), spec(2), spec(3), spec(3), spec(4), spec(2), spec(3),
            spec(4), spec(2), P("y", None, None, None), P("y", None),
        ),
        out_specs=P(ALL, None),
        check_vma=False,
    )
```
